256 devices in a mesh: energy: 16 (over x, y), domain: 16 (over z, core).
Axes of the slice: x: 4, y: 4, z: 8, core: 2. Of those that a mesh axis runs over, the one named last changes fastest.
Arguments:
- retarded: bfloat16 [16, 32, 256, 512], P('energy', 'domain'), may hold values from -1 to 2
- coupling: bfloat16 [32, 256, 512], P('domain'), may hold values from -1 to 2
- sigma_lesser: bfloat16 [16, 32, 256, 512], P('energy', 'domain'), may hold values from -4 to 4
- sigma_greater: bfloat16 [16, 32, 256, 512], P('energy', 'domain'), may hold values from -4 to 4
- tiles: int32 [32, 2], P('domain'), may hold values from 0 to 3, all different within a row
- offsets: int32 [16], replicated, may hold values from -8 to 8, as said below
Outputs:
- polarization: bfloat16 [16, 32, 2, 128, 256], P('energy', 'domain')
The draws below stay inside these ranges and needn't reach their ends.
Inputs may be any that keep to these rules, and one draw needn't show every extreme that they name: Each row names 2 different tiles. `offsets`: both ends of the range occur in every draw.
All inputs are finite; a program needn't handle non-finite values.
Results may differ from the reference program's by a relative error of at most 0.039.
Values may be sent and summed in bfloat16 or wider, within the bound.
A program may use at most 64 MiB of HBM per device.

```python
import jax
import jax.numpy as jnp
from jax import lax

B = 256
TILES = 4
TSEL = 2
NE = 16
TRANSPORT_BLOCKS = 32


energy_spread = 0.2


def draw_retarded(key, part):
    rate_key = jax.random.fold_in(key, 11)
    pulse_random_key = jax.random.fold_in(key, 12)
    jitter_key = jax.random.fold_in(key, 13)
    lowest = jnp.log(0.5 / TRANSPORT_BLOCKS)
    highest = jnp.log(0.08)
    decay_losses = jnp.exp(jax.random.uniform(rate_key, (NE,), jnp.float32, lowest, highest))
    tile_positions = jax.random.randint(pulse_random_key, (3,), 0, TRANSPORT_BLOCKS)
    selected_hits = jnp.any(jnp.arange(TRANSPORT_BLOCKS)[:, None] == tile_positions[None, :], axis=1)
    pulse_events = jnp.where(selected_hits, jnp.sqrt(0.6), 1.0)
    scale_factors = jnp.exp(-energy_spread * energy_spread - 0.5 * decay_losses)[:, None] * pulse_events[None, :]
    jitter = jax.random.truncated_normal(jitter_key, -4.0, 4.0, (NE, TRANSPORT_BLOCKS, B, 2 * B), jnp.float32)
    eye_block = jnp.concatenate([jnp.eye(B, dtype=jnp.float32), jnp.zeros((B, B), jnp.float32)], axis=1)
    return (scale_factors[:, :, None, None] * (eye_block + energy_spread * jitter / jnp.sqrt(2.0 * B))).astype(jnp.bfloat16)


def draw_coupling(key, part):
    jitter_key = jax.random.fold_in(key, 21)
    jitter = jax.random.truncated_normal(jitter_key, -4.0, 4.0, (TRANSPORT_BLOCKS, B, 2 * B), jnp.float32)
    eye_block = jnp.concatenate([jnp.eye(B, dtype=jnp.float32), jnp.zeros((B, B), jnp.float32)], axis=1)
    return (eye_block + energy_spread * jitter / jnp.sqrt(2.0 * B)).astype(jnp.bfloat16)


def draw_offsets(key, part):
    value_key = jax.random.fold_in(key, 31)
    place_key = jax.random.fold_in(key, 32)
    lowest_offset = 0 - NE // 2
    highest_offset = NE // 2
    values = jax.random.randint(value_key, (NE,), lowest_offset, highest_offset + 1, jnp.int32)
    places = jax.random.permutation(place_key, NE)
    values = values.at[places[0]].set(lowest_offset)
    values = values.at[places[1]].set(highest_offset)
    return values.astype(jnp.int32)


def levels(own_key, dims, shards, smallest, largest):
    factor_of, own = 1.0, jax.random.fold_in(own_key, 6)
    for axis_at, parts in shards:
        steps = jnp.exp(jax.random.uniform(jax.random.fold_in(own, axis_at), (parts,), jnp.float32, smallest / len(shards), largest / len(shards)))
        factor_of = factor_of * jnp.repeat(steps, dims[axis_at] // parts).reshape([-1 if axis == axis_at else 1 for axis in range(len(dims))])
    return factor_of


def picks_of(own_key, rows, number_of, top, lift):
    order = jax.random.permutation(jax.random.fold_in(own_key, 1), number_of)
    boost = order
    for power in range(3):
        boost = boost * boost // number_of
    boost = boost * lift // number_of
    tickets = jax.random.randint(jax.random.fold_in(own_key, 2), (rows, number_of), 0, 4096) + boost
    holders = jax.random.permutation(jax.random.fold_in(own_key, 3), rows)[jnp.arange(number_of) % rows]
    tickets = jnp.where(jnp.arange(rows)[:, None] == holders[None, :], 1 << 14, tickets)
    score = tickets * number_of + jnp.arange(number_of)
    return lax.top_k(score.astype(jnp.int32), top)[1].astype(jnp.int32)


def centred(rng, extent, spread, reach, split=(), kind=jnp.bfloat16):
    array = jax.random.normal(rng, extent, jnp.float32) * spread
    if len(split) > 0:
        array = levels(rng, extent, split, -0.22, 0.18) * array
    return jnp.clip(array, min=-reach, max=reach).astype(kind)


def setup_inputs(seed: int = 0) -> dict:
    arg_keys = jax.random.split(jax.random.key(seed), 7)
    retarded = draw_retarded(jax.random.fold_in(arg_keys[6], 71), 0)
    coupling = draw_coupling(jax.random.fold_in(arg_keys[6], 71), 0)
    sigma_lesser = centred(arg_keys[2], (NE, TRANSPORT_BLOCKS, B, 2 * B), 0.5, 4.0, ((0, 16), (1, 16)))
    sigma_greater = centred(arg_keys[3], (NE, TRANSPORT_BLOCKS, B, 2 * B), 0.5, 4.0, ((0, 16), (1, 16)))
    tiles = picks_of(arg_keys[4], TRANSPORT_BLOCKS, TILES, TSEL, 0)
    offsets = draw_offsets(jax.random.fold_in(arg_keys[6], 71), 0)
    return dict(retarded=retarded, coupling=coupling, sigma_lesser=sigma_lesser, sigma_greater=sigma_greater, tiles=tiles, offsets=offsets)


def stacked(block):
    block_order = block.shape[-2]
    real_part = block[..., :block_order]
    imag_part = block[..., block_order:]
    bottom = jnp.concatenate([-imag_part, real_part], axis=-1)
    return jnp.concatenate([block, bottom], axis=-2)


def product(factor, second):
    return jnp.matmul(factor.astype(jnp.float32), stacked(second).astype(jnp.float32))


def product_adjoint(factor, second):
    return jnp.matmul(factor.astype(jnp.float32), jnp.swapaxes(stacked(second), -1, -2).astype(jnp.float32))


def to_tiles(block, tile_rows):
    leading = block.shape[:-2]
    leading_count = len(leading)
    pieces = block.reshape(leading + (2, tile_rows, 2, 2, tile_rows))
    axes_order = tuple(range(leading_count)) + (leading_count, leading_count + 3, leading_count + 1, leading_count + 2, leading_count + 4)
    return pieces.transpose(axes_order).reshape(leading + (4, tile_rows, 2 * tile_rows))


def convolve(less_tiles, great_tiles, offsets):
    energies = less_tiles.shape[0]
    tile_rows = less_tiles.shape[-1] // 2
    pad_shape = (energies,) + great_tiles.shape[1:]
    padding = jnp.zeros(pad_shape, great_tiles.dtype)
    padded = jnp.concatenate([padding, great_tiles, padding], axis=0)

    def one_output(offset):
        begin_at = (energies - offset).astype(jnp.int32)
        shifted = lax.dynamic_slice_in_dim(padded, begin_at, energies, 0).astype(jnp.float32)
        less_real = less_tiles[..., :tile_rows].astype(jnp.float32)
        less_imag = less_tiles[..., tile_rows:].astype(jnp.float32)
        great_real = shifted[..., :tile_rows]
        great_imag = shifted[..., tile_rows:]
        out_real = jnp.sum(less_real * great_real - less_imag * great_imag, axis=0)
        out_imag = jnp.sum(less_real * great_imag + less_imag * great_real, axis=0)
        return (jnp.concatenate([out_real, out_imag], axis=-1) / energies).astype(jnp.bfloat16)

    return lax.map(one_output, offsets)


def sweep_step(states, inputs):
    lesser, greater = states
    retarded_block, coupling_block, lesser_source, greater_source, chosen = inputs
    propagator = product(retarded_block, coupling_block).astype(jnp.bfloat16)
    injected_less = product_adjoint(product(retarded_block, lesser_source).astype(jnp.bfloat16), retarded_block).astype(jnp.bfloat16)
    injected_great = product_adjoint(product(retarded_block, greater_source).astype(jnp.bfloat16), retarded_block).astype(jnp.bfloat16)
    lesser = (product_adjoint(product(propagator, lesser).astype(jnp.bfloat16), propagator) + injected_less.astype(jnp.float32)).astype(jnp.bfloat16)
    greater = (product_adjoint(product(propagator, greater).astype(jnp.bfloat16), propagator) + injected_great.astype(jnp.float32)).astype(jnp.bfloat16)
    tile_rows = lesser.shape[-2] // 2
    less_tiles = jnp.take(to_tiles(lesser, tile_rows), chosen, axis=1)
    great_tiles = jnp.take(to_tiles(greater, tile_rows), chosen, axis=1)
    return (lesser, greater), (less_tiles, great_tiles)


def reference(retarded, coupling, sigma_lesser, sigma_greater, tiles, offsets):
    empty_state = jnp.zeros((NE, B, 2 * B), jnp.bfloat16)
    inputs = (jnp.swapaxes(retarded, 0, 1), coupling, jnp.swapaxes(sigma_lesser, 0, 1), jnp.swapaxes(sigma_greater, 0, 1), tiles)
    _, (less_tiles, great_tiles) = lax.scan(sweep_step, (empty_state, empty_state), inputs)
    less_tiles = jnp.swapaxes(less_tiles, 0, 1)
    great_tiles = jnp.swapaxes(great_tiles, 0, 1)
    return convolve(less_tiles, great_tiles, offsets)
```

```python
import jax
import jax.numpy as jnp
from jax import lax
from jax.experimental import pallas as pl
from jax.experimental.pallas import tpu as pltpu
from jax.sharding import PartitionSpec as P

MESH = pl.DeviceIdType.MESH
BF = jnp.bfloat16
F32 = jnp.float32


def stacked(x):
    n = x.shape[1] // 2
    re, im = x[:, :n], x[:, n:]
    return jnp.concatenate([x, jnp.concatenate([-im, re], axis=1)], axis=0)


def mul(a, x):
    return jnp.dot(a, stacked(x), preferred_element_type=F32)


def mul_adj(y, a):
    return lax.dot_general(y, stacked(a), (((1,), (1,)), ((), ())), preferred_element_type=F32)


def congruence(t, s):
    return mul_adj(mul(t, s).astype(BF), t)


def kernel(ret, cpl, sl, sg, tiles_hbm, offs, out,
           R, C, SG, PP, T, J, JX, Q, A1, A2, S1, S2, S3, TB, SB, AB, LF, GF, OB, tl,
           ld, sp, rp, sj, rj, sa, ra, ss, rs, st, rt, sx, rx, so, ro):
    e = lax.axis_index("energy")
    d = lax.axis_index("domain")
    c, q = lax.div(d, 2), lax.rem(d, 2)
    peer = 2 * c + 1 - q

    def remote(src, dst, send, recv, ee, dd):
        return pltpu.make_async_remote_copy(src_ref=src, dst_ref=dst, send_sem=send, recv_sem=recv,
                                            device_id=(ee, dd), device_id_type=MESH)

    def at_chip(k):
        return 2 * k + q

    bar = pltpu.get_barrier_semaphore()
    for k in range(1, 8):
        pl.semaphore_signal(bar, 1, device_id=(e, at_chip(lax.rem(c + k, 8))), device_id_type=MESH)
    pl.semaphore_signal(bar, 1, device_id=(e, peer), device_id_type=MESH)
    for k in range(1, 16):
        for z in range(2):
            pl.semaphore_signal(bar, 1, device_id=(lax.rem(e + k, 16), 2 * c + z), device_id_type=MESH)

    loads = []
    for b in range(2):
        for n, (src, dst) in enumerate(((ret.at[0, b], R.at[b]), (cpl.at[b], C.at[b]),
                                        (sl.at[0, b], SG.at[0, b]), (sg.at[0, b], SG.at[1, b]))):
            cp = pltpu.make_async_copy(src, dst, ld.at[4 * b + n])
            cp.start()
            loads.append(cp)
    own_tiles = pltpu.make_async_copy(tiles_hbm, tl.at[q], ld.at[8])
    own_tiles.start()

    for b in range(2):
        loads[4 * b].wait()
        loads[4 * b + 1].wait()
        PP[2 * q + b] = mul(R[b], C[b]).astype(BF)
    pl.semaphore_wait(bar, 7 + 1 + 30)
    p_copy = remote(PP.at[pl.ds(2 * q, 2)], PP.at[pl.ds(2 * q, 2)], sp, rp, e, peer)
    p_copy.start()
    own_tiles.wait()
    t_copy = remote(tl.at[q], tl.at[q], st.at[1], rt.at[1], e, peer)
    t_copy.start()

    for b in range(2):
        loads[4 * b + 2].wait()
        loads[4 * b + 3].wait()
        JX[b] = mul_adj(mul(R[b], SG[1 - q, b]).astype(BF), R[b]).astype(BF)
    j_copy = remote(JX, J.at[pl.ds(2 * q, 2)], sj, rj, e, peer)
    j_copy.start()
    for b in range(2):
        J[2 * q + b] = mul_adj(mul(R[b], SG[q, b]).astype(BF), R[b]).astype(BF)

    p_copy.wait_recv()
    T[0] = PP[0]
    for i in range(1, 4):
        T[i] = mul(PP[i], T[i - 1]).astype(BF)
    half = pl.ds(pl.multiple_of(128 * q, 128), 128)
    a1 = remote(T.at[3, half], A1.at[half], sa.at[0], ra.at[0], e, at_chip(lax.rem(c + 1, 8)))
    a1f = remote(A1.at[half], A1.at[half], sa.at[1], ra.at[1], e, peer)
    a1_sender = (lax.rem(c, 2) == 0) & (c > 0)
    a1_taker = (lax.rem(c, 2) == 1) & (c > 1)

    @pl.when(a1_sender)
    def _():
        a1.start()

    j_copy.wait_recv()
    Q[0] = J[0]
    for i in range(1, 4):
        Q[i] = (congruence(PP[i], Q[i - 1]) + J[i].astype(F32)).astype(BF)

    even = lax.rem(c, 2) == 0
    s1 = remote(Q.at[3], S1, ss.at[0], rs.at[0], e, at_chip(lax.rem(c + 1, 8)))

    @pl.when(even)
    def _():
        s1.start()

    def update(i, slot, s_ref):
        Q[i] = (Q[i].astype(F32) + congruence(T[4 * slot + i], s_ref[...])).astype(BF)

    a2a = remote(T.at[7, half], A2.at[half], sa.at[2], ra.at[2], e, at_chip(lax.rem(c + 2, 8)))
    a2b = remote(T.at[7, half], A2.at[half], sa.at[3], ra.at[2], e, at_chip(lax.rem(c + 1, 8)))
    a2f = remote(A2.at[half], A2.at[half], sa.at[4], ra.at[3], e, peer)

    @pl.when(a1_taker)
    def _():
        a1.wait_recv()
        a1f.start()
        a1f.wait_recv()
        a_in = stacked(A1[...])
        for i in (3, 0, 1, 2):
            T[4 + i] = jnp.dot(T[i], a_in, preferred_element_type=F32).astype(BF)
            if i == 3:
                @pl.when(c == 5)
                def _():
                    a2a.start()
                    a2b.start()

    s2a = remote(Q.at[3], S2, ss.at[1], rs.at[1], e, at_chip(lax.rem(c + 2, 8)))
    s2b = remote(Q.at[3], S2, ss.at[2], rs.at[1], e, at_chip(lax.rem(c + 1, 8)))
    s2_sender = (c == 1) | (c == 5)

    @pl.when(jnp.logical_not(even))
    def _():
        s1.wait_recv()
        update(3, 0, S1)

        @pl.when(s2_sender)
        def _():
            s2a.start()
            s2b.start()

        for i in range(3):
            update(i, 0, S1)

    slot2 = lax.rem(c, 2)

    @pl.when(c >= 6)
    def _():
        a2a.wait_recv()
        a2f.start()
        a2f.wait_recv()
        a_in = stacked(A2[...])
        for i in range(4):
            T[8 + i] = jnp.dot(T[4 * slot2 + i], a_in, preferred_element_type=F32).astype(BF)

    @pl.when(even)
    def _():
        s1.wait_send()

    s3a = remote(Q.at[3], S3, ss.at[3], rs.at[2], e, at_chip(lax.rem(c + 2, 8)))
    s3b = remote(Q.at[3], S3, ss.at[4], rs.at[2], e, at_chip(lax.rem(c + 4, 8)))
    s3c = remote(S3, S3, ss.at[3], rs.at[2], e, at_chip(lax.rem(c + 1, 8)))
    s3d = remote(S3, S3, ss.at[4], rs.at[2], e, at_chip(lax.rem(c + 7, 8)))

    @pl.when(lax.rem(lax.div(c, 2), 2) == 1)
    def _():
        s2a.wait_recv()
        update(3, slot2, S2)

        @pl.when(c == 3)
        def _():
            s3a.start()
            s3b.start()

        for i in range(3):
            update(i, slot2, S2)

    @pl.when(s2_sender)
    def _():
        s2a.wait_send()
        s2b.wait_send()

    slot3 = jnp.where(c >= 6, 2, slot2)

    @pl.when(c >= 4)
    def _():
        s3a.wait_recv()

        @pl.when(c == 5)
        def _():
            s3c.start()
            s3d.start()

        for i in range(4):
            update(i, slot3, S3)

    t_copy.wait_recv()
    for i in range(4):
        for t in range(4):
            row, col = 128 * (t // 2), 128 * (t % 2)
            TB[4 * i + t, :, 0:128] = Q[i, row:row + 128, col:col + 128]
            TB[4 * i + t, :, 128:256] = Q[i, row:row + 128, col + 256:col + 384]
    for i in range(4):
        for j in range(2):
            tile = TB[4 * i + tl[i // 2, i % 2, j]]
            for r in range(4):
                SB[8 * i + 4 * j + r] = tile[32 * r:32 * r + 32]

    mine = pltpu.make_async_copy(SB.at[2 * e + q], AB.at[q, e], rx)
    mine.start()
    remote(SB.at[2 * e + 1 - q], AB.at[q, e], sx, rx, e, peer).start()
    for k in range(1, 16):
        o = lax.rem(e + k, 16)
        for z in range(2):
            remote(SB.at[2 * o + z], AB.at[q, e], sx, rx, o, 2 * c + z).start()
    GF[0:8] = jnp.zeros((8, 32, 256), F32)
    GF[24:32] = jnp.zeros((8, 32, 256), F32)
    pltpu.make_async_copy(AB, AB, rx).wait()
    pltpu.make_async_copy(SB.at[pl.ds(0, 31)], SB.at[pl.ds(0, 31)], sx).wait()

    for k in range(16):
        GF[8 + k] = AB[1, k].astype(F32)
    for rr in range(4):
        rows = pl.ds(8 * rr, 8)
        lr, li = [], []
        for k in range(16):
            v = AB[0, k, pl.ds(8 * rr, 8), :].astype(F32)
            lr.append(v[:, :128])
            li.append(v[:, 128:])
        for k in range(16):
            LF[k, rows, :] = jnp.concatenate([lr[k], li[k]], axis=1)

    def one(m, carry):
        base = 8 - offs[m]
        for rr in range(4):
            rows = pl.ds(8 * rr, 8)
            acc_r = jnp.zeros((8, 128), F32)
            acc_i = jnp.zeros((8, 128), F32)
            for k in range(16):
                lr = LF[k, rows, 0:128]
                li = LF[k, rows, 128:256]
                gr = GF[base + k, rows, 0:128]
                gi = GF[base + k, rows, 128:256]
                acc_r = acc_r + (lr * gr - li * gi)
                acc_i = acc_i + (lr * gi + li * gr)
            OB[m, rows, 0:128] = (acc_r * (1.0 / 16)).astype(BF)
            OB[m, rows, 128:256] = (acc_i * (1.0 / 16)).astype(BF)
        return carry

    lax.fori_loop(0, 16, one, 0)

    u, h = lax.div(e, 2), lax.rem(e, 2)
    blk, j = lax.div(u, 2), lax.rem(u, 2)
    home = lax.div(blk, 2)
    dst = out.at[0, lax.rem(blk, 2), j, pl.ds(pl.multiple_of(h * 64 + q * 32, 32), 32), :]
    is_home = home == q

    @pl.when(is_home)
    def _():
        pltpu.make_async_copy(OB.at[e], dst, ro).start()

    @pl.when(jnp.logical_not(is_home))
    def _():
        remote(OB.at[e], dst, so, ro, e, peer).start()

    for k in range(1, 16):
        m = lax.rem(e + k, 16)
        remote(OB.at[m], dst, so, ro, m, 2 * c + home).start()
    pltpu.make_async_copy(out, out, ro).wait()

    @pl.when(is_home)
    def _():
        pltpu.make_async_copy(OB.at[pl.ds(0, 15)], OB.at[pl.ds(0, 15)], so).wait()

    @pl.when(jnp.logical_not(is_home))
    def _():
        pltpu.make_async_copy(OB, OB, so).wait()

    p_copy.wait_send()
    t_copy.wait_send()
    j_copy.wait_send()

    @pl.when(a1_sender)
    def _():
        a1.wait_send()

    @pl.when(a1_taker)
    def _():
        a1f.wait_send()

    @pl.when(c == 5)
    def _():
        a2a.wait_send()
        a2b.wait_send()
        s3c.wait_send()
        s3d.wait_send()

    @pl.when(c >= 6)
    def _():
        a2f.wait_send()

    @pl.when(c == 3)
    def _():
        s3a.wait_send()
        s3b.wait_send()


def shards(retarded, coupling, sigma_lesser, sigma_greater, tiles, offsets):
    mat = (256, 512)
    dma = pltpu.SemaphoreType.DMA
    anyspace = pl.BlockSpec(memory_space=pltpu.HBM)
    return pl.pallas_call(
        kernel,
        out_shape=jax.ShapeDtypeStruct((1, 2, 2, 128, 256), BF),
        in_specs=[anyspace] * 5 + [pl.BlockSpec(memory_space=pltpu.SMEM)],
        out_specs=pl.BlockSpec(memory_space=pltpu.VMEM),
        scratch_shapes=[
            pltpu.VMEM((2,) + mat, BF), pltpu.VMEM((2,) + mat, BF), pltpu.VMEM((2, 2) + mat, BF),
            pltpu.VMEM((4,) + mat, BF), pltpu.VMEM((12,) + mat, BF), pltpu.VMEM((4,) + mat, BF),
            pltpu.VMEM((2,) + mat, BF), pltpu.VMEM((4,) + mat, BF),
            pltpu.VMEM(mat, BF), pltpu.VMEM(mat, BF),
            pltpu.VMEM(mat, BF), pltpu.VMEM(mat, BF), pltpu.VMEM(mat, BF),
            pltpu.VMEM((16, 128, 256), BF), pltpu.VMEM((32, 32, 256), BF), pltpu.VMEM((2, 16, 32, 256), BF),
            pltpu.VMEM((16, 32, 256), F32), pltpu.VMEM((32, 32, 256), F32), pltpu.VMEM((16, 32, 256), BF),
            pltpu.SMEM((2, 2, 2), jnp.int32),
            dma((9,)), dma, dma, dma, dma, dma((5,)), dma((4,)), dma((5,)), dma((3,)), dma((2,)), dma((2,)),
            dma, dma, dma, dma,
        ],
        compiler_params=pltpu.CompilerParams(
            collective_id=0, has_side_effects=True, vmem_limit_bytes=48 << 20),
        name="recursion",
    )(retarded, coupling, sigma_lesser, sigma_greater, tiles, offsets)


def solution(mesh):
    placed = (
        P("energy", "domain", None, None),
        P("domain", None, None),
        P("energy", "domain", None, None),
        P("energy", "domain", None, None),
        P("domain", None),
        P(),
    )
    return jax.shard_map(
        shards,
        mesh=mesh,
        in_specs=placed,
        out_specs=P("energy", "domain", None, None, None),
        check_vma=False,
    )
```

```python
import jax
import jax.numpy as jnp
from jax import lax
from jax.experimental import pallas as pl
from jax.experimental.pallas import tpu as pltpu
from jax.sharding import PartitionSpec as P

MESH = pl.DeviceIdType.MESH
BF = jnp.bfloat16
F32 = jnp.float32


def stacked(x):
    n = x.shape[1] // 2
    re, im = x[:, :n], x[:, n:]
    return jnp.concatenate([x, jnp.concatenate([-im, re], axis=1)], axis=0)


def mul(a, x):
    return jnp.dot(a, stacked(x), preferred_element_type=F32)


def mul_adj(y, a):
    return lax.dot_general(y, stacked(a), (((1,), (1,)), ((), ())), preferred_element_type=F32)


def congruence(t, s):
    return mul_adj(mul(t, s).astype(BF), t)


def kernel(ret, cpl, sl, sg, tiles_hbm, offs, out,
           R, C, SG, PP, T, J, JX, Q, A1, A2, S1, S2, S3, AD, SD, SE, ZB, X3, TB, SB, AB, LF, GF, OB, tl,
           ld, sp, rp, sj, rj, sa, ra, ss, rs, sd, rd, st, rt, sx3, rx3, sx, rx, so, ro):
    e = lax.axis_index("energy")
    d = lax.axis_index("domain")
    c, q = lax.div(d, 2), lax.rem(d, 2)
    peer = 2 * c + 1 - q

    def remote(src, dst, send, recv, ee, dd):
        return pltpu.make_async_remote_copy(src_ref=src, dst_ref=dst, send_sem=send, recv_sem=recv,
                                            device_id=(ee, dd), device_id_type=MESH)

    def at_chip(k):
        return 2 * k + q

    loads = []
    for b in range(2):
        for n, (src, dst) in enumerate(((ret.at[0, b], R.at[b]), (cpl.at[b], C.at[b]),
                                        (sl.at[0, b], SG.at[0, b]), (sg.at[0, b], SG.at[1, b]))):
            cp = pltpu.make_async_copy(src, dst, ld.at[4 * b + n])
            cp.start()
            loads.append(cp)
    own_tiles = pltpu.make_async_copy(tiles_hbm, tl.at[q], ld.at[8])
    own_tiles.start()

    bar = pltpu.get_barrier_semaphore()
    for k in range(1, 8):
        pl.semaphore_signal(bar, 1, device_id=(e, at_chip(lax.rem(c + k, 8))), device_id_type=MESH)
    pl.semaphore_signal(bar, 1, device_id=(e, peer), device_id_type=MESH)
    for k in range(1, 16):
        for z in range(2):
            pl.semaphore_signal(bar, 1, device_id=(lax.rem(e + k, 16), 2 * c + z), device_id_type=MESH)

    for b in range(2):
        loads[4 * b].wait()
        loads[4 * b + 1].wait()
        PP[2 * q + b] = mul(R[b], C[b]).astype(BF)
    pl.semaphore_wait(bar, 7 + 1 + 30)
    p_copy = remote(PP.at[pl.ds(2 * q, 2)], PP.at[pl.ds(2 * q, 2)], sp, rp, e, peer)
    p_copy.start()
    own_tiles.wait()
    t_copy = remote(tl.at[q], tl.at[q], st.at[1], rt.at[1], e, peer)
    t_copy.start()

    for b in range(2):
        loads[4 * b + 2].wait()
        loads[4 * b + 3].wait()
        JX[b] = mul_adj(mul(R[b], SG[1 - q, b]).astype(BF), R[b]).astype(BF)
    j_copy = remote(JX, J.at[pl.ds(2 * q, 2)], sj, rj, e, peer)
    j_copy.start()
    for b in range(2):
        J[2 * q + b] = mul_adj(mul(R[b], SG[q, b]).astype(BF), R[b]).astype(BF)

    even = lax.rem(c, 2) == 0
    rows2 = (pl.ds(0, 128), pl.ds(128, 128))
    low_greater = (c < 4) & (q == 1)
    below = at_chip(lax.rem(c + 7, 8))
    down_sender = low_greater & jnp.logical_not(even)
    down_taker = low_greater & even
    ad = remote(T.at[3], AD, sd.at[0], rd.at[0], e, below)

    p_copy.wait_recv()
    T[0] = PP[0]
    for i in range(1, 4):
        T[i] = mul(PP[i], T[i - 1]).astype(BF)
    half = pl.ds(pl.multiple_of(128 * q, 128), 128)
    a1 = remote(T.at[3, half], A1.at[half], sa.at[0], ra.at[0], e, at_chip(lax.rem(c + 1, 8)))
    a1f = remote(A1.at[half], A1.at[half], sa.at[1], ra.at[1], e, peer)
    a1_sender = (lax.rem(c, 2) == 0) & (c > 0)
    a1_taker = (lax.rem(c, 2) == 1) & (c > 1)

    @pl.when(a1_sender)
    def _():
        a1.start()

    @pl.when(down_sender)
    def _():
        ad.start()

    j_copy.wait_recv()
    Q[0] = J[0]
    for i in range(1, 4):
        Q[i] = (congruence(PP[i], Q[i - 1]) + J[i].astype(F32)).astype(BF)

    s1 = remote(Q.at[3], S1, ss.at[0], rs.at[0], e, at_chip(lax.rem(c + 1, 8)))

    dn = remote(Q.at[3], SD, sd.at[1], rd.at[1], e, below)
    ae = remote(A2, A2, sd.at[2], rd.at[2], e, at_chip(lax.rem(c + 6, 8)))
    ze = remote(ZB, SE, sd.at[3], rd.at[3], e, at_chip(lax.rem(c + 6, 8)))
    z2 = [remote(ZB.at[r], S2.at[r], ss.at[2 * n + 1 + p], rs.at[1 + p], e, at_chip(lax.rem(c + dist, 8)))
          for n, dist in enumerate((3, 2)) for p, r in enumerate(rows2)]

    def chip_at(distance):
        return at_chip(lax.rem(c + distance * (1 - 2 * q) + 16, 8))

    x3 = [[remote(X3.at[r], S3.at[r], sx3.at[2 * n + p], rx3.at[p], e, chip_at(dist)) for p, r in enumerate(rows2)]
          for n, dist in enumerate((3, 2, 1))]
    hop = [remote(S3.at[r], S3.at[r], sx3.at[p], rx3.at[p], e, chip_at(1)) for p, r in enumerate(rows2)]
    relay = c == jnp.where(q == 0, 6, 5)

    @pl.when(even & jnp.logical_not(low_greater))
    def _():
        s1.start()

    @pl.when(down_sender)
    def _():
        dn.start()

    @pl.when(down_taker)
    def _():
        ad.wait_recv()

        @pl.when(c == 2)
        def _():
            A2[...] = mul(AD[...], T[3]).astype(BF)
            ae.start()

        dn.wait_recv()
        ZB[...] = (congruence(AD[...], Q[3]) + SD[...].astype(F32)).astype(BF)

        @pl.when(c == 2)
        def _():
            ze.start()
            ze.wait_send()

        s1.start()

        @pl.when(c == 0)
        def _():
            ae.wait_recv()
            for cp in z2:
                cp.start()
            ze.wait_recv()
            X3[...] = (congruence(A2[...], ZB[...]) + SE[...].astype(F32)).astype(BF)
            for to in x3:
                for cp in to:
                    cp.start()

    def update(i, slot, s_ref):
        Q[i] = (Q[i].astype(F32) + congruence(T[4 * slot + i], s_ref[...])).astype(BF)

    a2b = remote(T.at[7, half], A2.at[half], sa.at[2], ra.at[2], e, at_chip(lax.rem(c + 1, 8)))
    a2r = remote(A2.at[half], A2.at[half], sa.at[3], ra.at[2], e, at_chip(lax.rem(c + 1, 8)))
    a2f = remote(A2.at[half], A2.at[half], sa.at[4], ra.at[3], e, peer)

    @pl.when(a1_taker)
    def _():
        a1.wait_recv()
        a1f.start()
        a1f.wait_recv()
        a_in = stacked(A1[...])
        for i in (3, 0, 1, 2):
            T[4 + i] = jnp.dot(T[i], a_in, preferred_element_type=F32).astype(BF)
            if i == 3:
                @pl.when(c == 5)
                def _():
                    a2b.start()

    s2_low = (c == 1) & (q == 0)
    far = at_chip(lax.rem(c + jnp.where(c == 1, 2, 1), 8))
    s2a = [remote(Q.at[3, r], S2.at[r], ss.at[1 + p], rs.at[1 + p], e, far) for p, r in enumerate(rows2)]
    s2b = [remote(Q.at[3, r], S2.at[r], ss.at[3 + p], rs.at[1 + p], e, at_chip(lax.rem(c + 1, 8)))
           for p, r in enumerate(rows2)]
    s2r = [remote(S2.at[r], S2.at[r], ss.at[1 + p], rs.at[1 + p], e, at_chip(lax.rem(c + 1, 8)))
           for p, r in enumerate(rows2)]
    s2_sender = s2_low | (c == 5)

    @pl.when(jnp.logical_not(even))
    def _():
        s1.wait_recv()

        @pl.when(down_sender)
        def _():
            dn.wait_send()

        update(3, 0, S1)

        @pl.when(s2_sender)
        def _():
            for cp in s2a:
                cp.start()

        for i in range(3):
            update(i, 0, S1)

        @pl.when(s2_sender)
        def _():
            for cp in s2a:
                cp.wait_send()

        @pl.when(s2_low)
        def _():
            for cp in s2b:
                cp.start()

    slot2 = lax.rem(c, 2)

    @pl.when(c >= 6)
    def _():
        a2b.wait_recv()
        a2f.start()

        @pl.when(c == 6)
        def _():
            a2r.start()

        a2f.wait_recv()
        a_in = stacked(A2[...])
        for i in range(4):
            T[8 + i] = jnp.dot(T[4 * slot2 + i], a_in, preferred_element_type=F32).astype(BF)

    @pl.when(even)
    def _():
        s1.wait_send()

    @pl.when(lax.rem(lax.div(c, 2), 2) == 1)
    def _():
        for cp, on in zip(s2a, s2r):
            cp.wait_recv()

            @pl.when(c == 6)
            def _(on=on):
                on.start()

        update(3, slot2, S2)

        @pl.when((c == 3) & (q == 0))
        def _():
            X3[...] = Q[3]
            for to in x3:
                for cp in to:
                    cp.start()

        for i in range(3):
            update(i, slot2, S2)

    @pl.when(s2_low)
    def _():
        for cp in s2b:
            cp.wait_send()

    slot3 = jnp.where(c >= 6, 2, slot2)

    @pl.when(c >= 4)
    def _():
        for cp in hop:
            cp.wait_recv()

            @pl.when(relay)
            def _(cp=cp):
                cp.start()

    t_copy.wait_recv()
    ex, ey = lax.div(e, 4), lax.rem(e, 4)
    for i in range(4):
        @pl.when(c >= 4)
        def _(i=i):
            update(i, slot3, S3)

        for t in range(4):
            row, col = 128 * (t // 2), 128 * (t % 2)
            TB[4 * i + t, :, 0:128] = Q[i, row:row + 128, col:col + 128]
            TB[4 * i + t, :, 128:256] = Q[i, row:row + 128, col + 256:col + 384]
        for j in range(2):
            tile = TB[4 * i + tl[i // 2, i % 2, j]]
            for r in range(4):
                SB[8 * i + 4 * j + r] = tile[32 * r:32 * r + 32]
        for w in range(4):
            owner = 4 * w + (w + i) % 4
            here = e == owner
            for z in range(2):
                piece = SB.at[8 * i + 2 * w + z]

                @pl.when(jnp.logical_not(here))
                def _(piece=piece, owner=owner, z=z):
                    remote(piece, AB.at[q, e], sx, rx, owner, 2 * c + z).start()

            @pl.when(here)
            def _(i=i, w=w):
                pltpu.make_async_copy(SB.at[8 * i + 2 * w + q], AB.at[q, e], rx).start()
                remote(SB.at[8 * i + 2 * w + 1 - q], AB.at[q, e], sx, rx, e, peer).start()

    GF[0:8] = jnp.zeros((8, 32, 256), F32)
    GF[24:32] = jnp.zeros((8, 32, 256), F32)
    pltpu.make_async_copy(AB, AB, rx).wait()
    pltpu.make_async_copy(SB.at[pl.ds(0, 31)], SB.at[pl.ds(0, 31)], sx).wait()

    for k in range(16):
        GF[8 + k] = AB[1, k].astype(F32)
    for rr in range(4):
        rows = pl.ds(8 * rr, 8)
        lr, li = [], []
        for k in range(16):
            v = AB[0, k, pl.ds(8 * rr, 8), :].astype(F32)
            lr.append(v[:, :128])
            li.append(v[:, 128:])
        for k in range(16):
            LF[k, rows, :] = jnp.concatenate([lr[k], li[k]], axis=1)

    def one(m, carry):
        base = 8 - offs[m]
        for rr in range(4):
            rows = pl.ds(8 * rr, 8)
            acc_r = jnp.zeros((8, 128), F32)
            acc_i = jnp.zeros((8, 128), F32)
            for k in range(16):
                lr = LF[k, rows, 0:128]
                li = LF[k, rows, 128:256]
                gr = GF[base + k, rows, 0:128]
                gi = GF[base + k, rows, 128:256]
                acc_r = acc_r + (lr * gr - li * gi)
                acc_i = acc_i + (lr * gi + li * gr)
            OB[m, rows, 0:128] = (acc_r * (1.0 / 16)).astype(BF)
            OB[m, rows, 128:256] = (acc_i * (1.0 / 16)).astype(BF)
        return carry

    lax.fori_loop(0, 16, one, 0)

    blk, j, h = lax.rem(ey - ex + 4, 4), lax.div(ex, 2), lax.rem(ex, 2)
    home = lax.div(blk, 2)
    dst = out.at[0, lax.rem(blk, 2), j, pl.ds(pl.multiple_of(h * 64 + q * 32, 32), 32), :]
    is_home = home == q

    @pl.when(is_home)
    def _():
        pltpu.make_async_copy(OB.at[e], dst, ro).start()

    @pl.when(jnp.logical_not(is_home))
    def _():
        remote(OB.at[e], dst, so, ro, e, peer).start()

    for k in range(1, 16):
        m = lax.rem(e + k, 16)
        remote(OB.at[m], dst, so, ro, m, 2 * c + home).start()
    pltpu.make_async_copy(out, out, ro).wait()

    @pl.when(is_home)
    def _():
        pltpu.make_async_copy(OB.at[pl.ds(0, 15)], OB.at[pl.ds(0, 15)], so).wait()

    @pl.when(jnp.logical_not(is_home))
    def _():
        pltpu.make_async_copy(OB, OB, so).wait()

    p_copy.wait_send()
    t_copy.wait_send()
    j_copy.wait_send()

    @pl.when(a1_sender)
    def _():
        a1.wait_send()

    @pl.when(a1_taker)
    def _():
        a1f.wait_send()

    @pl.when(c == 5)
    def _():
        a2b.wait_send()

    @pl.when(c >= 6)
    def _():
        a2f.wait_send()

    @pl.when(c == 6)
    def _():
        a2r.wait_send()
        for cp in s2r:
            cp.wait_send()

    @pl.when(down_sender)
    def _():
        ad.wait_send()

    @pl.when(low_greater & (c == 2))
    def _():
        ae.wait_send()

    @pl.when(low_greater & (c == 0))
    def _():
        for cp in z2:
            cp.wait_send()

    @pl.when(c == jnp.where(q == 0, 3, 0))
    def _():
        for to in x3:
            for cp in to:
                cp.wait_send()

    @pl.when(relay)
    def _():
        for cp in hop:
            cp.wait_send()


def shards(retarded, coupling, sigma_lesser, sigma_greater, tiles, offsets):
    mat = (256, 512)
    dma = pltpu.SemaphoreType.DMA
    anyspace = pl.BlockSpec(memory_space=pltpu.HBM)
    return pl.pallas_call(
        kernel,
        out_shape=pltpu.VMEM((1, 2, 2, 128, 256), BF),
        in_specs=[anyspace] * 5 + [pl.BlockSpec(memory_space=pltpu.SMEM)],
        out_specs=pl.BlockSpec(memory_space=pltpu.VMEM),
        scratch_shapes=[
            pltpu.VMEM((2,) + mat, BF), pltpu.VMEM((2,) + mat, BF), pltpu.VMEM((2, 2) + mat, BF),
            pltpu.VMEM((4,) + mat, BF), pltpu.VMEM((12,) + mat, BF), pltpu.VMEM((4,) + mat, BF),
            pltpu.VMEM((2,) + mat, BF), pltpu.VMEM((4,) + mat, BF),
            pltpu.VMEM(mat, BF), pltpu.VMEM(mat, BF),
            pltpu.VMEM(mat, BF), pltpu.VMEM(mat, BF), pltpu.VMEM(mat, BF),
            pltpu.VMEM(mat, BF), pltpu.VMEM(mat, BF), pltpu.VMEM(mat, BF), pltpu.VMEM(mat, BF), pltpu.VMEM(mat, BF),
            pltpu.VMEM((16, 128, 256), BF), pltpu.VMEM((32, 32, 256), BF), pltpu.VMEM((2, 16, 32, 256), BF),
            pltpu.VMEM((16, 32, 256), F32), pltpu.VMEM((32, 32, 256), F32), pltpu.VMEM((16, 32, 256), BF),
            pltpu.SMEM((2, 2, 2), jnp.int32),
            dma((9,)), dma, dma, dma, dma, dma((5,)), dma((4,)), dma((5,)), dma((3,)), dma((4,)), dma((4,)),
            dma((2,)), dma((2,)), dma((6,)), dma((2,)), dma, dma, dma, dma,
        ],
        compiler_params=pltpu.CompilerParams(
            collective_id=0, has_side_effects=True, vmem_limit_bytes=63 << 20),
        name="recursion",
    )(retarded, coupling, sigma_lesser, sigma_greater, tiles, offsets)


def solution(mesh):
    placed = (
        P("energy", "domain", None, None),
        P("domain", None, None),
        P("energy", "domain", None, None),
        P("energy", "domain", None, None),
        P("domain", None),
        P(),
    )
    return jax.shard_map(
        shards,
        mesh=mesh,
        in_specs=placed,
        out_specs=P("energy", "domain", None, None, None),
        check_vma=False,
    )
```

```python
import jax
import jax.numpy as jnp
from jax import lax
from jax.experimental import pallas as pl
from jax.experimental.pallas import tpu as pltpu
from jax.sharding import PartitionSpec as P

MESH = pl.DeviceIdType.MESH
BF = jnp.bfloat16
F32 = jnp.float32


def stacked(x):
    n = x.shape[1] // 2
    re, im = x[:, :n], x[:, n:]
    return jnp.concatenate([x, jnp.concatenate([-im, re], axis=1)], axis=0)


def mul(a, x):
    return jnp.dot(a, stacked(x), preferred_element_type=F32)


def mul_adj(y, a):
    return lax.dot_general(y, stacked(a), (((1,), (1,)), ((), ())), preferred_element_type=F32)


def congruence(t, s):
    return mul_adj(mul(t, s).astype(BF), t)


def kernel(ret, cpl, sl, sg, tiles_hbm, offs, out,
           R, C, SG, PP, T, J, JX, Q, A1, A2, S1, S2, S3, AD, SD, SE, ZB, X3, TB, SB, AB, LF, GF, OB, tl,
           ld, sp, rp, sj, rj, sa, ra, ss, rs, sd, rd, st, rt, sx3, rx3, sx, rx, so, ro, go):
    e = lax.axis_index("energy")
    d = lax.axis_index("domain")
    c, q = lax.div(d, 2), lax.rem(d, 2)
    peer = 2 * c + 1 - q

    def remote(src, dst, send, recv, ee, dd):
        return pltpu.make_async_remote_copy(src_ref=src, dst_ref=dst, send_sem=send, recv_sem=recv,
                                            device_id=(ee, dd), device_id_type=MESH)

    def at_chip(k):
        return 2 * k + q

    loads = []
    for b in range(2):
        for n, (src, dst) in enumerate(((ret.at[0, b], R.at[b]), (cpl.at[b], C.at[b]),
                                        (sl.at[0, b], SG.at[0, b]), (sg.at[0, b], SG.at[1, b]))):
            cp = pltpu.make_async_copy(src, dst, ld.at[4 * b + n])
            cp.start()
            loads.append(cp)
    own_tiles = pltpu.make_async_copy(tiles_hbm, tl.at[q], ld.at[8])
    own_tiles.start()

    bar = pltpu.get_barrier_semaphore()
    low = c < 4
    base4 = 4 * lax.div(c, 4)
    source = jnp.where(q == 0, 3, 0)
    for k in range(1, 4):
        pl.semaphore_signal(bar, 1, device_id=(e, at_chip(base4 + lax.rem(c + k, 4))), device_id_type=MESH)
    pl.semaphore_signal(bar, 1, device_id=(e, peer), device_id_type=MESH)
    for k in range(1, 16):
        for z in range(2):
            pl.semaphore_signal(bar, 1, device_id=(lax.rem(e + k, 16), 2 * c + z), device_id_type=MESH)

    @pl.when(c == source)
    def _():
        for k in range(4, 8):
            pl.semaphore_signal(bar, 1, device_id=(e, at_chip(k)), device_id_type=MESH)

    for b in range(2):
        loads[4 * b].wait()
        loads[4 * b + 1].wait()
        PP[2 * q + b] = mul(R[b], C[b]).astype(BF)
    pl.semaphore_wait(bar, jnp.where(low, 34, 35))

    @pl.when(jnp.logical_not(low))
    def _():
        pl.semaphore_signal(go, 1, device_id=(e, at_chip(source)), device_id_type=MESH)

    p_copy = remote(PP.at[pl.ds(2 * q, 2)], PP.at[pl.ds(2 * q, 2)], sp, rp, e, peer)
    p_copy.start()
    own_tiles.wait()
    t_copy = remote(tl.at[q], tl.at[q], st.at[1], rt.at[1], e, peer)
    t_copy.start()

    for b in range(2):
        loads[4 * b + 2].wait()
        loads[4 * b + 3].wait()
        JX[b] = mul_adj(mul(R[b], SG[1 - q, b]).astype(BF), R[b]).astype(BF)
    j_copy = remote(JX, J.at[pl.ds(2 * q, 2)], sj, rj, e, peer)
    j_copy.start()
    for b in range(2):
        J[2 * q + b] = mul_adj(mul(R[b], SG[q, b]).astype(BF), R[b]).astype(BF)

    even = lax.rem(c, 2) == 0
    rows2 = [pl.ds(64 * p, 64) for p in range(4)]
    mirrored = (c < 4) & (q == 1)
    below = at_chip(lax.rem(c + 7, 8))
    down_sender = mirrored & jnp.logical_not(even)
    down_taker = mirrored & even
    ad = remote(T.at[3], AD, sd.at[0], rd.at[0], e, below)

    p_copy.wait_recv()
    T[0] = PP[0]
    for i in range(1, 4):
        T[i] = mul(PP[i], T[i - 1]).astype(BF)
    half = pl.ds(pl.multiple_of(128 * q, 128), 128)
    a1 = remote(T.at[3, half], A1.at[half], sa.at[0], ra.at[0], e, at_chip(lax.rem(c + 1, 8)))
    a1f = remote(A1.at[half], A1.at[half], sa.at[1], ra.at[1], e, peer)
    a1_sender = (lax.rem(c, 2) == 0) & (c > 0)
    a1_taker = (lax.rem(c, 2) == 1) & (c > 1)

    @pl.when(a1_sender)
    def _():
        a1.start()

    @pl.when(down_sender)
    def _():
        ad.start()

    j_copy.wait_recv()
    Q[0] = J[0]
    for i in range(1, 4):
        Q[i] = (congruence(PP[i], Q[i - 1]) + J[i].astype(F32)).astype(BF)

    s1 = remote(Q.at[3], S1, ss.at[0], rs.at[0], e, at_chip(lax.rem(c + 1, 8)))

    dn = remote(Q.at[3], SD, sd.at[1], rd.at[1], e, below)
    ae = remote(A2, A2, sd.at[2], rd.at[2], e, at_chip(lax.rem(c + 6, 8)))
    ze = remote(ZB, SE, sd.at[3], rd.at[3], e, at_chip(lax.rem(c + 6, 8)))
    z2 = [remote(ZB.at[r], S2.at[r], ss.at[4 * n + 1 + p], rs.at[1 + p], e, at_chip(lax.rem(c + dist, 8)))
          for n, dist in enumerate((3, 2)) for p, r in enumerate(rows2)]

    def chip_at(distance):
        return at_chip(lax.rem(c + distance * (1 - 2 * q) + 16, 8))

    x3 = [[remote(X3.at[r], S3.at[r], sx3.at[4 * n + p], rx3.at[p], e, chip_at(dist)) for p, r in enumerate(rows2)]
          for n, dist in enumerate((3, 1, 2))]
    hop = [remote(S3.at[r], S3.at[r], sx3.at[p], rx3.at[p], e, chip_at(1)) for p, r in enumerate(rows2)]
    relay = c == jnp.where(q == 0, 6, 5)

    @pl.when(even & jnp.logical_not(mirrored))
    def _():
        s1.start()
        s1.wait_send()

    @pl.when(down_sender)
    def _():
        dn.start()

    @pl.when(down_taker)
    def _():
        ad.wait_recv()

        @pl.when(c == 2)
        def _():
            A2[...] = mul(AD[...], T[3]).astype(BF)
            ae.start()

        dn.wait_recv()
        ZB[...] = (congruence(AD[...], Q[3]) + SD[...].astype(F32)).astype(BF)

        @pl.when(c == 2)
        def _():
            ze.start()
            ze.wait_send()

        s1.start()

        @pl.when(c == 0)
        def _():
            ae.wait_recv()
            for cp in z2:
                cp.start()
            ze.wait_recv()
            X3[...] = (congruence(A2[...], ZB[...]) + SE[...].astype(F32)).astype(BF)
            pl.semaphore_wait(go, 4)
            for to in x3:
                for cp in to:
                    cp.start()

    def update(i, slot, s_ref):
        Q[i] = (Q[i].astype(F32) + congruence(T[4 * slot + i], s_ref[...])).astype(BF)

    a2b = remote(T.at[7, half], A2.at[half], sa.at[2], ra.at[2], e, at_chip(lax.rem(c + 1, 8)))
    a2r = remote(A2.at[half], A2.at[half], sa.at[3], ra.at[2], e, at_chip(lax.rem(c + 1, 8)))
    a2f = remote(A2.at[half], A2.at[half], sa.at[4], ra.at[3], e, peer)

    def composites1():
        a1.wait_recv()
        a1f.start()
        a1f.wait_recv()
        a_in = stacked(A1[...])
        for i in (3, 0, 1, 2):
            T[4 + i] = jnp.dot(T[i], a_in, preferred_element_type=F32).astype(BF)
            if i == 3:
                @pl.when(c == 5)
                def _():
                    a2b.start()

    @pl.when(a1_taker)
    def _():
        composites1()

    s2_low = (c == 1) & (q == 0)
    s2_sender = ((c == 1) & (q == 0)) | (c == 5)
    far = at_chip(lax.rem(c + jnp.where(c == 1, 2, 1), 8))
    s2a = [remote(Q.at[3, r], S2.at[r], ss.at[1 + p], rs.at[1 + p], e, far) for p, r in enumerate(rows2)]
    s2b = [remote(Q.at[3, r], S2.at[r], ss.at[5 + p], rs.at[1 + p], e, at_chip(lax.rem(c + 1, 8)))
           for p, r in enumerate(rows2)]
    s2r = [remote(S2.at[r], S2.at[r], ss.at[1 + p], rs.at[1 + p], e, at_chip(lax.rem(c + 1, 8)))
           for p, r in enumerate(rows2)]

    @pl.when(jnp.logical_not(even))
    def _():
        s1.wait_recv()

        @pl.when(down_sender)
        def _():
            dn.wait_send()

        update(3, 0, S1)

        @pl.when(s2_sender)
        def _():
            for cp in s2a:
                cp.start()

        for i in range(3):
            update(i, 0, S1)

        @pl.when(s2_sender)
        def _():
            for cp in s2a:
                cp.wait_send()

        @pl.when(s2_low)
        def _():
            for cp in s2b:
                cp.start()

    slot2 = lax.rem(c, 2)

    @pl.when(c >= 6)
    def _():
        a2b.wait_recv()

        a2f.start()

        @pl.when(c == 6)
        def _():
            a2r.start()

        a2f.wait_recv()

    @pl.when(even & mirrored)
    def _():
        s1.wait_send()

    @pl.when(lax.rem(lax.div(c, 2), 2) == 1)
    def _():
        for cp, on in zip(s2a, s2r):
            cp.wait_recv()

            @pl.when(c == 6)
            def _(on=on):
                on.start()

    @pl.when((c == 2) | (c == 3))
    def _():
        update(3, slot2, S2)

        @pl.when((c == 3) & (q == 0))
        def _():
            X3[...] = Q[3]
            pl.semaphore_wait(go, 4)
            for cp in x3[0]:
                cp.start()

        for i in range(3):
            update(i, slot2, S2)

        @pl.when((c == 3) & (q == 0))
        def _():
            for to in x3[1:]:
                for cp in to:
                    cp.start()

    @pl.when(s2_low)
    def _():
        for cp in s2b:
            cp.wait_send()


    @pl.when(c >= 4)
    def _():
        for cp in hop:
            cp.wait_recv()

            @pl.when(relay)
            def _(cp=cp):
                cp.start()

    @pl.when(c >= 6)
    def _():
        SE[...] = (congruence(A2[...], S3[...]) + S2[...].astype(F32)).astype(BF)

    @pl.when((c == 4) | (c == 5))
    def _():
        SE[...] = S3[...]

    t_copy.wait_recv()
    ex, ey = lax.div(e, 4), lax.rem(e, 4)
    for i in range(4):
        @pl.when(c >= 4)
        def _(i=i):
            update(i, slot2, SE)

        for t in range(4):
            row, col = 128 * (t // 2), 128 * (t % 2)
            TB[4 * i + t, :, 0:128] = Q[i, row:row + 128, col:col + 128]
            TB[4 * i + t, :, 128:256] = Q[i, row:row + 128, col + 256:col + 384]
        for j in range(2):
            tile = TB[4 * i + tl[i // 2, i % 2, j]]
            for r in range(4):
                SB[8 * i + 4 * j + r] = tile[32 * r:32 * r + 32]
        here = lax.rem(ex + i, 4) == ey
        for a in (2, 1, 3, 0):
            w = lax.rem(ex + a, 4)
            owner = 4 * w + lax.rem(w + i, 4)

            def send(i=i, w=w, owner=owner):
                for z in range(2):
                    remote(SB.at[8 * i + 2 * w + z], AB.at[q, e], sx, rx, owner, 2 * c + z).start()

            if a:
                send()
            else:
                pl.when(jnp.logical_not(here))(send)

                @pl.when(here)
                def _(i=i, w=w):
                    pltpu.make_async_copy(SB.at[8 * i + 2 * w + q], AB.at[q, e], rx).start()
                    remote(SB.at[8 * i + 2 * w + 1 - q], AB.at[q, e], sx, rx, e, peer).start()

    GF[0:8] = jnp.zeros((8, 32, 256), F32)
    GF[24:32] = jnp.zeros((8, 32, 256), F32)
    pltpu.make_async_copy(AB, AB, rx).wait()
    pltpu.make_async_copy(SB.at[pl.ds(0, 31)], SB.at[pl.ds(0, 31)], sx).wait()

    for k in range(16):
        GF[8 + k] = AB[1, k].astype(F32)
    for rr in range(4):
        rows = pl.ds(8 * rr, 8)
        lr, li = [], []
        for k in range(16):
            v = AB[0, k, pl.ds(8 * rr, 8), :].astype(F32)
            lr.append(v[:, :128])
            li.append(v[:, 128:])
        for k in range(16):
            LF[k, rows, :] = jnp.concatenate([lr[k], li[k]], axis=1)

    blk, j, h = lax.rem(ey - ex + 4, 4), lax.div(ex, 2), lax.rem(ex, 2)
    home = lax.div(blk, 2)
    dst = out.at[0, lax.rem(blk, 2), j, pl.ds(pl.multiple_of(h * 64 + q * 32, 32), 32), :]
    is_home = home == q

    def far_first(k):
        return jnp.where(k == 3, 0, jnp.where(k == 0, 2, 2 * k - 1))

    def one(n, carry):
        ma = lax.rem(ex + far_first(lax.div(n, 4)), 4)
        mb = lax.rem(ey + far_first(lax.rem(n, 4)), 4)
        m = 4 * ma + mb
        base = 8 - offs[m]
        for rr in range(4):
            rows = pl.ds(8 * rr, 8)
            acc_r = jnp.zeros((8, 128), F32)
            acc_i = jnp.zeros((8, 128), F32)
            for k in range(16):
                lr = LF[k, rows, 0:128]
                li = LF[k, rows, 128:256]
                gr = GF[base + k, rows, 0:128]
                gi = GF[base + k, rows, 128:256]
                acc_r = acc_r + (lr * gr - li * gi)
                acc_i = acc_i + (lr * gi + li * gr)
            OB[m, rows, 0:128] = (acc_r * (1.0 / 16)).astype(BF)
            OB[m, rows, 128:256] = (acc_i * (1.0 / 16)).astype(BF)

        @pl.when(n < 15)
        def _():
            remote(OB.at[m], dst, so, ro, m, 2 * c + home).start()

        return carry

    lax.fori_loop(0, 16, one, 0)

    @pl.when(is_home)
    def _():
        pltpu.make_async_copy(OB.at[e], dst, ro).start()

    @pl.when(jnp.logical_not(is_home))
    def _():
        remote(OB.at[e], dst, so, ro, e, peer).start()

    pltpu.make_async_copy(out, out, ro).wait()

    @pl.when(is_home)
    def _():
        pltpu.make_async_copy(OB.at[pl.ds(0, 15)], OB.at[pl.ds(0, 15)], so).wait()

    @pl.when(jnp.logical_not(is_home))
    def _():
        pltpu.make_async_copy(OB, OB, so).wait()

    p_copy.wait_send()
    t_copy.wait_send()
    j_copy.wait_send()

    @pl.when(a1_sender)
    def _():
        a1.wait_send()

    @pl.when(a1_taker)
    def _():
        a1f.wait_send()

    @pl.when(c == 5)
    def _():
        a2b.wait_send()

    @pl.when(c >= 6)
    def _():
        a2f.wait_send()

    @pl.when(c == 6)
    def _():
        a2r.wait_send()
        for cp in s2r:
            cp.wait_send()

    @pl.when(down_sender)
    def _():
        ad.wait_send()

    @pl.when(mirrored & (c == 2))
    def _():
        ae.wait_send()

    @pl.when(mirrored & (c == 0))
    def _():
        for cp in z2:
            cp.wait_send()

    @pl.when(c == source)
    def _():
        for to in x3:
            for cp in to:
                cp.wait_send()

    @pl.when(relay)
    def _():
        for cp in hop:
            cp.wait_send()


def shards(retarded, coupling, sigma_lesser, sigma_greater, tiles, offsets):
    mat = (256, 512)
    dma = pltpu.SemaphoreType.DMA
    anyspace = pl.BlockSpec(memory_space=pltpu.HBM)
    return pl.pallas_call(
        kernel,
        out_shape=pltpu.VMEM((1, 2, 2, 128, 256), BF),
        in_specs=[anyspace] * 5 + [pl.BlockSpec(memory_space=pltpu.SMEM)],
        out_specs=pl.BlockSpec(memory_space=pltpu.VMEM),
        scratch_shapes=[
            pltpu.VMEM((2,) + mat, BF), pltpu.VMEM((2,) + mat, BF), pltpu.VMEM((2, 2) + mat, BF),
            pltpu.VMEM((4,) + mat, BF), pltpu.VMEM((8,) + mat, BF), pltpu.VMEM((4,) + mat, BF),
            pltpu.VMEM((2,) + mat, BF), pltpu.VMEM((4,) + mat, BF),
            pltpu.VMEM(mat, BF), pltpu.VMEM(mat, BF),
            pltpu.VMEM(mat, BF), pltpu.VMEM(mat, BF), pltpu.VMEM(mat, BF),
            pltpu.VMEM(mat, BF), pltpu.VMEM(mat, BF), pltpu.VMEM(mat, BF), pltpu.VMEM(mat, BF), pltpu.VMEM(mat, BF),
            pltpu.VMEM((16, 128, 256), BF), pltpu.VMEM((32, 32, 256), BF), pltpu.VMEM((2, 16, 32, 256), BF),
            pltpu.VMEM((16, 32, 256), F32), pltpu.VMEM((32, 32, 256), F32), pltpu.VMEM((16, 32, 256), BF),
            pltpu.SMEM((2, 2, 2), jnp.int32),
            dma((9,)), dma, dma, dma, dma, dma((5,)), dma((4,)), dma((9,)), dma((5,)), dma((4,)), dma((4,)),
            dma((2,)), dma((2,)), dma((12,)), dma((4,)), dma, dma, dma, dma, pltpu.SemaphoreType.REGULAR,
        ],
        compiler_params=pltpu.CompilerParams(
            collective_id=0, has_side_effects=True, vmem_limit_bytes=63 << 20),
        name="recursion",
    )(retarded, coupling, sigma_lesser, sigma_greater, tiles, offsets)


def solution(mesh):
    placed = (
        P("energy", "domain", None, None),
        P("domain", None, None),
        P("energy", "domain", None, None),
        P("energy", "domain", None, None),
        P("domain", None),
        P(),
    )
    return jax.shard_map(
        shards,
        mesh=mesh,
        in_specs=placed,
        out_specs=P("energy", "domain", None, None, None),
        check_vma=False,
    )
```

```python
import jax
import jax.numpy as jnp
from jax import lax
from jax.experimental import pallas as pl
from jax.experimental.pallas import tpu as pltpu
from jax.sharding import PartitionSpec as P

MESH = pl.DeviceIdType.MESH
BF = jnp.bfloat16
F32 = jnp.float32


def stacked(x):
    n = x.shape[1] // 2
    re, im = x[:, :n], x[:, n:]
    return jnp.concatenate([x, jnp.concatenate([-im, re], axis=1)], axis=0)


def mul(a, x):
    return jnp.dot(a, stacked(x), preferred_element_type=F32)


def mul_adj(y, a):
    return lax.dot_general(y, stacked(a), (((1,), (1,)), ((), ())), preferred_element_type=F32)


def congruence(t, s):
    return mul_adj(mul(t, s).astype(BF), t)


def kernel(ret, cpl, sl, sg, tiles_hbm, offs, out,
           R, C, SG, PP, T, J, JX, Q, A1, A2, S1, S2, S3, AD, SD, SE, ZB, X3, TB, SB, AB, LF, GF, OB, tl,
           ld, sp, rp, sj, rj, sa, ra, ss, rs, sd, rd, st, rt, sx3, rx3, sx, rx, so, ro, go):
    e = lax.axis_index("energy")
    d = lax.axis_index("domain")
    c, q = lax.div(d, 2), lax.rem(d, 2)
    peer = 2 * c + 1 - q

    def remote(src, dst, send, recv, ee, dd):
        return pltpu.make_async_remote_copy(src_ref=src, dst_ref=dst, send_sem=send, recv_sem=recv,
                                            device_id=(ee, dd), device_id_type=MESH)

    def at_chip(k):
        return 2 * k + q

    loads = []
    for b in range(2):
        for n, (src, dst) in enumerate(((ret.at[0, b], R.at[b]), (cpl.at[b], C.at[b]),
                                        (sl.at[0, b], SG.at[0, b]), (sg.at[0, b], SG.at[1, b]))):
            cp = pltpu.make_async_copy(src, dst, ld.at[4 * b + n])
            cp.start()
            loads.append(cp)
    own_tiles = pltpu.make_async_copy(tiles_hbm, tl.at[q], ld.at[8])
    own_tiles.start()

    bar = pltpu.get_barrier_semaphore()
    low = c < 4
    base4 = 4 * lax.div(c, 4)
    source = jnp.where(q == 0, 3, 0)
    for k in range(1, 4):
        pl.semaphore_signal(bar, 1, device_id=(e, at_chip(base4 + lax.rem(c + k, 4))), device_id_type=MESH)
    pl.semaphore_signal(bar, 1, device_id=(e, peer), device_id_type=MESH)
    for k in range(1, 16):
        for z in range(2):
            pl.semaphore_signal(bar, 1, device_id=(lax.rem(e + k, 16), 2 * c + z), device_id_type=MESH)

    @pl.when(c == source)
    def _():
        for k in range(4, 8):
            pl.semaphore_signal(bar, 1, device_id=(e, at_chip(k)), device_id_type=MESH)

    for b in range(2):
        loads[4 * b].wait()
        loads[4 * b + 1].wait()
        PP[2 * q + b] = mul(R[b], C[b]).astype(BF)
    pl.semaphore_wait(bar, jnp.where(low, 34, 35))

    @pl.when(jnp.logical_not(low))
    def _():
        pl.semaphore_signal(go, 1, device_id=(e, at_chip(source)), device_id_type=MESH)

    p_copy = remote(PP.at[pl.ds(2 * q, 2)], PP.at[pl.ds(2 * q, 2)], sp, rp, e, peer)
    p_copy.start()
    own_tiles.wait()
    t_copy = remote(tl.at[q], tl.at[q], st.at[1], rt.at[1], e, peer)
    t_copy.start()

    for b in range(2):
        loads[4 * b + 2].wait()
        loads[4 * b + 3].wait()
        JX[b] = mul_adj(mul(R[b], SG[1 - q, b]).astype(BF), R[b]).astype(BF)
    j_copy = remote(JX, J.at[pl.ds(2 * q, 2)], sj, rj, e, peer)
    j_copy.start()
    for b in range(2):
        J[2 * q + b] = mul_adj(mul(R[b], SG[q, b]).astype(BF), R[b]).astype(BF)

    even = lax.rem(c, 2) == 0
    rows2 = [pl.ds(64 * p, 64) for p in range(4)]
    mirrored = (c < 4) & (q == 1)
    below = at_chip(lax.rem(c + 7, 8))
    down_sender = mirrored & jnp.logical_not(even)
    down_taker = mirrored & even
    ad = remote(T.at[3], AD, sd.at[0], rd.at[0], e, below)

    p_copy.wait_recv()
    T[0] = PP[0]
    for i in range(1, 4):
        T[i] = mul(PP[i], T[i - 1]).astype(BF)
    half = pl.ds(pl.multiple_of(128 * q, 128), 128)
    a1 = remote(T.at[3, half], A1.at[half], sa.at[0], ra.at[0], e, at_chip(lax.rem(c + 1, 8)))
    a1f = remote(A1.at[half], A1.at[half], sa.at[1], ra.at[1], e, peer)
    a1_sender = (lax.rem(c, 2) == 0) & (c > 0)
    a1_taker = (lax.rem(c, 2) == 1) & (c > 1)

    @pl.when(a1_sender)
    def _():
        a1.start()

    @pl.when(down_sender)
    def _():
        ad.start()

    j_copy.wait_recv()
    Q[0] = J[0]
    for i in range(1, 4):
        Q[i] = (congruence(PP[i], Q[i - 1]) + J[i].astype(F32)).astype(BF)

    s1 = remote(Q.at[3], S1, ss.at[0], rs.at[0], e, at_chip(lax.rem(c + 1, 8)))

    dn = remote(Q.at[3], SD, sd.at[1], rd.at[1], e, below)
    ae = remote(A2, A2, sd.at[2], rd.at[2], e, at_chip(lax.rem(c + 6, 8)))
    ze = remote(ZB, SE, sd.at[3], rd.at[3], e, at_chip(lax.rem(c + 6, 8)))
    z2 = [remote(ZB.at[r], S2.at[r], ss.at[4 * n + 1 + p], rs.at[1 + p], e, at_chip(lax.rem(c + dist, 8)))
          for n, dist in enumerate((3, 2)) for p, r in enumerate(rows2)]

    def chip_at(distance):
        return at_chip(lax.rem(c + distance * (1 - 2 * q) + 16, 8))

    x3 = [[remote(X3.at[r], S3.at[r], sx3.at[4 * n + p], rx3.at[p], e, chip_at(dist)) for p, r in enumerate(rows2)]
          for n, dist in enumerate((3, 4, 1, 2))]
    hop = [remote(S3.at[r], S3.at[r], sx3.at[p], rx3.at[p], e, chip_at(1)) for p, r in enumerate(rows2)]

    @pl.when(even & jnp.logical_not(mirrored))
    def _():
        s1.start()
        s1.wait_send()

    @pl.when(down_sender)
    def _():
        dn.start()

    @pl.when(down_taker)
    def _():
        ad.wait_recv()

        @pl.when(c == 2)
        def _():
            A2[...] = mul(AD[...], T[3]).astype(BF)
            ae.start()

        dn.wait_recv()
        ZB[...] = (congruence(AD[...], Q[3]) + SD[...].astype(F32)).astype(BF)

        @pl.when(c == 2)
        def _():
            ze.start()
            ze.wait_send()

        s1.start()

        @pl.when(c == 0)
        def _():
            ae.wait_recv()
            for cp in z2:
                cp.start()
            ze.wait_recv()
            X3[...] = (congruence(A2[...], ZB[...]) + SE[...].astype(F32)).astype(BF)
            pl.semaphore_wait(go, 4)
            for to in x3:
                for cp in to:
                    cp.start()

    def update(i, slot, s_ref):
        Q[i] = (Q[i].astype(F32) + congruence(T[4 * slot + i], s_ref[...])).astype(BF)

    a2b = remote(T.at[7, half], A2.at[half], sa.at[2], ra.at[2], e, at_chip(lax.rem(c + 1, 8)))
    a2r = remote(A2.at[half], A2.at[half], sa.at[3], ra.at[2], e, at_chip(lax.rem(c + 1, 8)))
    a2f = remote(A2.at[half], A2.at[half], sa.at[4], ra.at[3], e, peer)

    def composites1():
        a1.wait_recv()
        a1f.start()
        a1f.wait_recv()
        a_in = stacked(A1[...])
        for i in (3, 0, 1, 2):
            T[4 + i] = jnp.dot(T[i], a_in, preferred_element_type=F32).astype(BF)
            if i == 3:
                @pl.when(c == 5)
                def _():
                    a2b.start()

    @pl.when(a1_taker)
    def _():
        composites1()

    s2_low = (c == 1) & (q == 0)
    s2_sender = ((c == 1) & (q == 0)) | (c == 5)
    far = at_chip(lax.rem(c + jnp.where(c == 1, 2, 1), 8))
    s2a = [remote(Q.at[3, r], S2.at[r], ss.at[1 + p], rs.at[1 + p], e, far) for p, r in enumerate(rows2)]
    s2b = [remote(Q.at[3, r], S2.at[r], ss.at[5 + p], rs.at[1 + p], e, at_chip(lax.rem(c + 1, 8)))
           for p, r in enumerate(rows2)]
    s2r = [remote(S2.at[r], S2.at[r], ss.at[1 + p], rs.at[1 + p], e, at_chip(lax.rem(c + 1, 8)))
           for p, r in enumerate(rows2)]

    @pl.when(jnp.logical_not(even))
    def _():
        s1.wait_recv()

        @pl.when(down_sender)
        def _():
            dn.wait_send()

        update(3, 0, S1)

        @pl.when(s2_sender)
        def _():
            for cp in s2a:
                cp.start()

        for i in range(3):
            update(i, 0, S1)

        @pl.when(s2_sender)
        def _():
            for cp in s2a:
                cp.wait_send()

        @pl.when(s2_low)
        def _():
            for cp in s2b:
                cp.start()

    slot2 = lax.rem(c, 2)

    @pl.when(c >= 6)
    def _():
        a2b.wait_recv()

        a2f.start()

        @pl.when(c == 6)
        def _():
            a2r.start()

        a2f.wait_recv()

    @pl.when(even & mirrored)
    def _():
        s1.wait_send()

    @pl.when(lax.rem(lax.div(c, 2), 2) == 1)
    def _():
        for cp, on in zip(s2a, s2r):
            cp.wait_recv()

            @pl.when(c == 6)
            def _(on=on):
                on.start()

    @pl.when((c == 2) | (c == 3))
    def _():
        update(3, slot2, S2)

        @pl.when((c == 3) & (q == 0))
        def _():
            X3[...] = Q[3]
            pl.semaphore_wait(go, 4)
            for cp in x3[0]:
                cp.start()

        for i in range(3):
            update(i, slot2, S2)

        @pl.when((c == 3) & (q == 0))
        def _():
            for to in x3[1:]:
                for cp in to:
                    cp.start()

    @pl.when(s2_low)
    def _():
        for cp in s2b:
            cp.wait_send()


    @pl.when(c >= 4)
    def _():
        for cp in hop:
            cp.wait_recv()

    @pl.when(c >= 6)
    def _():
        SE[...] = (congruence(A2[...], S3[...]) + S2[...].astype(F32)).astype(BF)

    @pl.when((c == 4) | (c == 5))
    def _():
        SE[...] = S3[...]

    t_copy.wait_recv()
    ex, ey = lax.div(e, 4), lax.rem(e, 4)
    for i in range(4):
        @pl.when(c >= 4)
        def _(i=i):
            update(i, slot2, SE)

        for t in range(4):
            row, col = 128 * (t // 2), 128 * (t % 2)
            TB[4 * i + t, :, 0:128] = Q[i, row:row + 128, col:col + 128]
            TB[4 * i + t, :, 128:256] = Q[i, row:row + 128, col + 256:col + 384]
        for j in range(2):
            tile = TB[4 * i + tl[i // 2, i % 2, j]]
            for r in range(4):
                SB[8 * i + 4 * j + r] = tile[32 * r:32 * r + 32]
        here = lax.rem(ex + i, 4) == ey
        for a in (2, 1, 3, 0):
            w = lax.rem(ex + a, 4)
            owner = 4 * w + lax.rem(w + i, 4)

            def send(i=i, w=w, owner=owner):
                for z in range(2):
                    remote(SB.at[8 * i + 2 * w + z], AB.at[q, e], sx, rx, owner, 2 * c + z).start()

            if a:
                send()
            else:
                pl.when(jnp.logical_not(here))(send)

                @pl.when(here)
                def _(i=i, w=w):
                    pltpu.make_async_copy(SB.at[8 * i + 2 * w + q], AB.at[q, e], rx).start()
                    remote(SB.at[8 * i + 2 * w + 1 - q], AB.at[q, e], sx, rx, e, peer).start()

    GF[0:8] = jnp.zeros((8, 32, 256), F32)
    GF[24:32] = jnp.zeros((8, 32, 256), F32)
    pltpu.make_async_copy(AB, AB, rx).wait()
    pltpu.make_async_copy(SB.at[pl.ds(0, 31)], SB.at[pl.ds(0, 31)], sx).wait()

    for k in range(16):
        GF[8 + k] = AB[1, k].astype(F32)
    for rr in range(4):
        rows = pl.ds(8 * rr, 8)
        lr, li = [], []
        for k in range(16):
            v = AB[0, k, pl.ds(8 * rr, 8), :].astype(F32)
            lr.append(v[:, :128])
            li.append(v[:, 128:])
        for k in range(16):
            LF[k, rows, :] = jnp.concatenate([lr[k], li[k]], axis=1)

    blk, j, h = lax.rem(ey - ex + 4, 4), lax.div(ex, 2), lax.rem(ex, 2)
    home = lax.div(blk, 2)
    dst = out.at[0, lax.rem(blk, 2), j, pl.ds(pl.multiple_of(h * 64 + q * 32, 32), 32), :]
    is_home = home == q

    def far_first(k):
        return jnp.where(k == 3, 0, jnp.where(k == 0, 2, 2 * k - 1))

    def one(n, carry):
        ma = lax.rem(ex + far_first(lax.div(n, 4)), 4)
        mb = lax.rem(ey + far_first(lax.rem(n, 4)), 4)
        m = 4 * ma + mb
        base = 8 - offs[m]
        for rr in range(4):
            rows = pl.ds(8 * rr, 8)
            acc_r = jnp.zeros((8, 128), F32)
            acc_i = jnp.zeros((8, 128), F32)
            for k in range(16):
                lr = LF[k, rows, 0:128]
                li = LF[k, rows, 128:256]
                gr = GF[base + k, rows, 0:128]
                gi = GF[base + k, rows, 128:256]
                acc_r = acc_r + (lr * gr - li * gi)
                acc_i = acc_i + (lr * gi + li * gr)
            OB[m, rows, 0:128] = (acc_r * (1.0 / 16)).astype(BF)
            OB[m, rows, 128:256] = (acc_i * (1.0 / 16)).astype(BF)

        @pl.when(n < 15)
        def _():
            remote(OB.at[m], dst, so, ro, m, 2 * c + home).start()

        return carry

    lax.fori_loop(0, 16, one, 0)

    @pl.when(is_home)
    def _():
        pltpu.make_async_copy(OB.at[e], dst, ro).start()

    @pl.when(jnp.logical_not(is_home))
    def _():
        remote(OB.at[e], dst, so, ro, e, peer).start()

    pltpu.make_async_copy(out, out, ro).wait()

    @pl.when(is_home)
    def _():
        pltpu.make_async_copy(OB.at[pl.ds(0, 15)], OB.at[pl.ds(0, 15)], so).wait()

    @pl.when(jnp.logical_not(is_home))
    def _():
        pltpu.make_async_copy(OB, OB, so).wait()

    p_copy.wait_send()
    t_copy.wait_send()
    j_copy.wait_send()

    @pl.when(a1_sender)
    def _():
        a1.wait_send()

    @pl.when(a1_taker)
    def _():
        a1f.wait_send()

    @pl.when(c == 5)
    def _():
        a2b.wait_send()

    @pl.when(c >= 6)
    def _():
        a2f.wait_send()

    @pl.when(c == 6)
    def _():
        a2r.wait_send()
        for cp in s2r:
            cp.wait_send()

    @pl.when(down_sender)
    def _():
        ad.wait_send()

    @pl.when(mirrored & (c == 2))
    def _():
        ae.wait_send()

    @pl.when(mirrored & (c == 0))
    def _():
        for cp in z2:
            cp.wait_send()

    @pl.when(c == source)
    def _():
        for to in x3:
            for cp in to:
                cp.wait_send()


def shards(retarded, coupling, sigma_lesser, sigma_greater, tiles, offsets):
    mat = (256, 512)
    dma = pltpu.SemaphoreType.DMA
    anyspace = pl.BlockSpec(memory_space=pltpu.HBM)
    return pl.pallas_call(
        kernel,
        out_shape=pltpu.VMEM((1, 2, 2, 128, 256), BF),
        in_specs=[anyspace] * 5 + [pl.BlockSpec(memory_space=pltpu.SMEM)],
        out_specs=pl.BlockSpec(memory_space=pltpu.VMEM),
        scratch_shapes=[
            pltpu.VMEM((2,) + mat, BF), pltpu.VMEM((2,) + mat, BF), pltpu.VMEM((2, 2) + mat, BF),
            pltpu.VMEM((4,) + mat, BF), pltpu.VMEM((8,) + mat, BF), pltpu.VMEM((4,) + mat, BF),
            pltpu.VMEM((2,) + mat, BF), pltpu.VMEM((4,) + mat, BF),
            pltpu.VMEM(mat, BF), pltpu.VMEM(mat, BF),
            pltpu.VMEM(mat, BF), pltpu.VMEM(mat, BF), pltpu.VMEM(mat, BF),
            pltpu.VMEM(mat, BF), pltpu.VMEM(mat, BF), pltpu.VMEM(mat, BF), pltpu.VMEM(mat, BF), pltpu.VMEM(mat, BF),
            pltpu.VMEM((16, 128, 256), BF), pltpu.VMEM((32, 32, 256), BF), pltpu.VMEM((2, 16, 32, 256), BF),
            pltpu.VMEM((16, 32, 256), F32), pltpu.VMEM((32, 32, 256), F32), pltpu.VMEM((16, 32, 256), BF),
            pltpu.SMEM((2, 2, 2), jnp.int32),
            dma((9,)), dma, dma, dma, dma, dma((5,)), dma((4,)), dma((9,)), dma((5,)), dma((4,)), dma((4,)),
            dma((2,)), dma((2,)), dma((16,)), dma((4,)), dma, dma, dma, dma, pltpu.SemaphoreType.REGULAR,
        ],
        compiler_params=pltpu.CompilerParams(
            collective_id=0, has_side_effects=True, vmem_limit_bytes=63 << 20),
        name="recursion",
    )(retarded, coupling, sigma_lesser, sigma_greater, tiles, offsets)


def solution(mesh):
    placed = (
        P("energy", "domain", None, None),
        P("domain", None, None),
        P("energy", "domain", None, None),
        P("energy", "domain", None, None),
        P("domain", None),
        P(),
    )
    return jax.shard_map(
        shards,
        mesh=mesh,
        in_specs=placed,
        out_specs=P("energy", "domain", None, None, None),
        check_vma=False,
    )
```

```python
import jax
import jax.numpy as jnp
from jax import lax
from jax.experimental import pallas as pl
from jax.experimental.pallas import tpu as pltpu
from jax.sharding import PartitionSpec as P

MESH = pl.DeviceIdType.MESH
BF = jnp.bfloat16
F32 = jnp.float32


def stacked(x):
    n = x.shape[1] // 2
    re, im = x[:, :n], x[:, n:]
    return jnp.concatenate([x, jnp.concatenate([-im, re], axis=1)], axis=0)


def mul(a, x):
    return jnp.dot(a, stacked(x), preferred_element_type=F32)


def mul_adj(y, a):
    return lax.dot_general(y, stacked(a), (((1,), (1,)), ((), ())), preferred_element_type=F32)


def congruence(t, s):
    return mul_adj(mul(t, s).astype(BF), t)


def kernel(ret, cpl, sl, sg, tiles_hbm, offs, out,
           R, C, SG, PP, T, J, JX, Q, A1, A2, S1, S2, S3, AD, SD, SE, ZB, X3, TB, SB, AB, LF, GF, OB, tl,
           ld, sp, rp, sj, rj, sa, ra, ss, rs, sd, rd, st, rt, sx3, rx3, sx, rx, so, ro, go):
    e = lax.axis_index("energy")
    d = lax.axis_index("domain")
    c, q = lax.div(d, 2), lax.rem(d, 2)
    peer = 2 * c + 1 - q

    def remote(src, dst, send, recv, ee, dd):
        return pltpu.make_async_remote_copy(src_ref=src, dst_ref=dst, send_sem=send, recv_sem=recv,
                                            device_id=(ee, dd), device_id_type=MESH)

    def at_chip(k):
        return 2 * k + q

    loads = []
    for b in range(2):
        for n, (src, dst) in enumerate(((ret.at[0, b], R.at[b]), (cpl.at[b], C.at[b]),
                                        (sl.at[0, b], SG.at[0, b]), (sg.at[0, b], SG.at[1, b]))):
            cp = pltpu.make_async_copy(src, dst, ld.at[4 * b + n])
            cp.start()
            loads.append(cp)
    own_tiles = pltpu.make_async_copy(tiles_hbm, tl.at[q], ld.at[8])
    own_tiles.start()

    bar = pltpu.get_barrier_semaphore()
    low = c < 4
    base4 = 4 * lax.div(c, 4)
    source = jnp.where(q == 0, 3, 0)
    for k in range(1, 4):
        pl.semaphore_signal(bar, 1, device_id=(e, at_chip(base4 + lax.rem(c + k, 4))), device_id_type=MESH)
    pl.semaphore_signal(bar, 1, device_id=(e, peer), device_id_type=MESH)
    for k in range(1, 16):
        for z in range(2):
            pl.semaphore_signal(bar, 1, device_id=(lax.rem(e + k, 16), 2 * c + z), device_id_type=MESH)

    @pl.when(c == source)
    def _():
        for k in range(4, 8):
            pl.semaphore_signal(bar, 1, device_id=(e, at_chip(k)), device_id_type=MESH)

    for b in range(2):
        loads[4 * b].wait()
        loads[4 * b + 1].wait()
        PP[2 * q + b] = mul(R[b], C[b]).astype(BF)
    pl.semaphore_wait(bar, jnp.where(low, 34, 35))

    @pl.when(jnp.logical_not(low))
    def _():
        pl.semaphore_signal(go, 1, device_id=(e, at_chip(source)), device_id_type=MESH)

    p_copy = remote(PP.at[pl.ds(2 * q, 2)], PP.at[pl.ds(2 * q, 2)], sp, rp, e, peer)
    p_copy.start()
    own_tiles.wait()
    t_copy = remote(tl.at[q], tl.at[q], st.at[1], rt.at[1], e, peer)
    t_copy.start()

    for b in range(2):
        loads[4 * b + 2].wait()
        loads[4 * b + 3].wait()
        JX[b] = mul_adj(mul(R[b], SG[1 - q, b]).astype(BF), R[b]).astype(BF)
    j_copy = remote(JX, J.at[pl.ds(2 * q, 2)], sj, rj, e, peer)
    j_copy.start()
    for b in range(2):
        J[2 * q + b] = mul_adj(mul(R[b], SG[q, b]).astype(BF), R[b]).astype(BF)

    even = lax.rem(c, 2) == 0
    rows2 = [pl.ds(64 * p, 64) for p in range(4)]
    mirrored = (c < 4) & (q == 1)
    below = at_chip(lax.rem(c + 7, 8))
    down_sender = mirrored & jnp.logical_not(even)
    down_taker = mirrored & even
    ad = remote(T.at[3], AD, sd.at[0], rd.at[0], e, below)

    p_copy.wait_recv()
    T[0] = PP[0]
    for i in range(1, 4):
        T[i] = mul(PP[i], T[i - 1]).astype(BF)
    half = pl.ds(pl.multiple_of(128 * q, 128), 128)
    a1 = remote(T.at[3, half], A1.at[half], sa.at[0], ra.at[0], e, at_chip(lax.rem(c + 1, 8)))
    a1f = remote(A1.at[half], A1.at[half], sa.at[1], ra.at[1], e, peer)
    a1_sender = (lax.rem(c, 2) == 0) & (c > 0)
    a1_taker = (lax.rem(c, 2) == 1) & (c > 1)

    @pl.when(a1_sender)
    def _():
        a1.start()

    @pl.when(down_sender)
    def _():
        ad.start()

    j_copy.wait_recv()
    Q[0] = J[0]
    for i in range(1, 4):
        Q[i] = (congruence(PP[i], Q[i - 1]) + J[i].astype(F32)).astype(BF)

    s1 = remote(Q.at[3], S1, ss.at[0], rs.at[0], e, at_chip(lax.rem(c + 1, 8)))

    dn = remote(Q.at[3], SD, sd.at[1], rd.at[1], e, below)
    ae = remote(A2, A2, sd.at[2], rd.at[2], e, at_chip(lax.rem(c + 6, 8)))
    ze = remote(ZB, SE, sd.at[3], rd.at[3], e, at_chip(lax.rem(c + 6, 8)))
    z2 = [remote(ZB.at[r], S2.at[r], ss.at[4 * n + 1 + p], rs.at[1 + p], e, at_chip(lax.rem(c + dist, 8)))
          for n, dist in enumerate((3, 2)) for p, r in enumerate(rows2)]

    def chip_at(distance):
        return at_chip(lax.rem(c + distance * (1 - 2 * q) + 16, 8))

    x3 = [[remote(X3.at[r], S3.at[r], sx3.at[4 * n + p], rx3.at[p], e, chip_at(dist)) for p, r in enumerate(rows2)]
          for n, dist in enumerate(jnp.where(q == 0, a, b) for a, b in zip((3, 4, 2, 1), (3, 1, 2, 4)))]
    hop = [remote(S3.at[r], S3.at[r], sx3.at[p], rx3.at[p], e, chip_at(1)) for p, r in enumerate(rows2)]

    @pl.when(even & jnp.logical_not(mirrored))
    def _():
        s1.start()
        s1.wait_send()

    @pl.when(down_sender)
    def _():
        dn.start()

    @pl.when(down_taker)
    def _():
        ad.wait_recv()

        @pl.when(c == 2)
        def _():
            A2[...] = mul(AD[...], T[3]).astype(BF)
            ae.start()

        dn.wait_recv()
        ZB[...] = (congruence(AD[...], Q[3]) + SD[...].astype(F32)).astype(BF)

        @pl.when(c == 2)
        def _():
            ze.start()
            ze.wait_send()

        s1.start()

        @pl.when(c == 0)
        def _():
            ae.wait_recv()
            for cp in z2:
                cp.start()
            ze.wait_recv()
            X3[...] = (congruence(A2[...], ZB[...]) + SE[...].astype(F32)).astype(BF)
            pl.semaphore_wait(go, 4)
            for to in x3:
                for cp in to:
                    cp.start()

    def update(i, slot, s_ref):
        Q[i] = (Q[i].astype(F32) + congruence(T[4 * slot + i], s_ref[...])).astype(BF)

    a2b = remote(T.at[7, half], A2.at[half], sa.at[2], ra.at[2], e, at_chip(lax.rem(c + 1, 8)))
    a2r = remote(A2.at[half], A2.at[half], sa.at[3], ra.at[2], e, at_chip(lax.rem(c + 1, 8)))
    a2f = remote(A2.at[half], A2.at[half], sa.at[4], ra.at[3], e, peer)

    def composites1():
        a1.wait_recv()
        a1f.start()
        a1f.wait_recv()
        a_in = stacked(A1[...])
        for i in (3, 0, 1, 2):
            T[4 + i] = jnp.dot(T[i], a_in, preferred_element_type=F32).astype(BF)
            if i == 3:
                @pl.when(c == 5)
                def _():
                    a2b.start()

    @pl.when(a1_taker)
    def _():
        composites1()

    s2_low = (c == 1) & (q == 0)
    s2_sender = ((c == 1) & (q == 0)) | (c == 5)
    far = at_chip(lax.rem(c + jnp.where(c == 1, 2, 1), 8))
    s2a = [remote(Q.at[3, r], S2.at[r], ss.at[1 + p], rs.at[1 + p], e, far) for p, r in enumerate(rows2)]
    s2b = [remote(Q.at[3, r], S2.at[r], ss.at[5 + p], rs.at[1 + p], e, at_chip(lax.rem(c + 1, 8)))
           for p, r in enumerate(rows2)]
    s2r = [remote(S2.at[r], S2.at[r], ss.at[1 + p], rs.at[1 + p], e, at_chip(lax.rem(c + 1, 8)))
           for p, r in enumerate(rows2)]

    @pl.when(jnp.logical_not(even))
    def _():
        s1.wait_recv()

        @pl.when(down_sender)
        def _():
            dn.wait_send()

        update(3, 0, S1)

        @pl.when(s2_sender)
        def _():
            for cp in s2a:
                cp.start()

        for i in range(3):
            update(i, 0, S1)

        @pl.when(s2_sender)
        def _():
            for cp in s2a:
                cp.wait_send()

        @pl.when(s2_low)
        def _():
            for cp in s2b:
                cp.start()

    slot2 = lax.rem(c, 2)

    @pl.when(c >= 6)
    def _():
        a2b.wait_recv()

        a2f.start()

        @pl.when(c == 6)
        def _():
            a2r.start()

        a2f.wait_recv()

    @pl.when(even & mirrored)
    def _():
        s1.wait_send()

    @pl.when(lax.rem(lax.div(c, 2), 2) == 1)
    def _():
        for cp, on in zip(s2a, s2r):
            cp.wait_recv()

            @pl.when(c == 6)
            def _(on=on):
                on.start()

    @pl.when((c == 2) | (c == 3))
    def _():
        update(3, slot2, S2)

        @pl.when((c == 3) & (q == 0))
        def _():
            X3[...] = Q[3]
            pl.semaphore_wait(go, 4)
            for cp in x3[0]:
                cp.start()

        for i in range(3):
            update(i, slot2, S2)

        @pl.when((c == 3) & (q == 0))
        def _():
            for to in x3[1:]:
                for cp in to:
                    cp.start()

    @pl.when(s2_low)
    def _():
        for cp in s2b:
            cp.wait_send()


    @pl.when(c >= 4)
    def _():
        for cp in hop:
            cp.wait_recv()

    @pl.when(c >= 6)
    def _():
        SE[...] = (congruence(A2[...], S3[...]) + S2[...].astype(F32)).astype(BF)

    @pl.when((c == 4) | (c == 5))
    def _():
        SE[...] = S3[...]

    t_copy.wait_recv()
    ex, ey = lax.div(e, 4), lax.rem(e, 4)
    for i in range(4):
        @pl.when(c >= 4)
        def _(i=i):
            update(i, slot2, SE)

        for t in range(4):
            row, col = 128 * (t // 2), 128 * (t % 2)
            TB[4 * i + t, :, 0:128] = Q[i, row:row + 128, col:col + 128]
            TB[4 * i + t, :, 128:256] = Q[i, row:row + 128, col + 256:col + 384]
        for j in range(2):
            tile = TB[4 * i + tl[i // 2, i % 2, j]]
            for r in range(4):
                SB[8 * i + 4 * j + r] = tile[32 * r:32 * r + 32]
        here = lax.rem(ex + i, 4) == ey
        for a in (2, 1, 3, 0):
            w = lax.rem(ex + a, 4)
            owner = 4 * w + lax.rem(w + i, 4)

            def send(i=i, w=w, owner=owner):
                for z in range(2):
                    remote(SB.at[8 * i + 2 * w + z], AB.at[q, e], sx, rx, owner, 2 * c + z).start()

            if a:
                send()
            else:
                pl.when(jnp.logical_not(here))(send)

                @pl.when(here)
                def _(i=i, w=w):
                    pltpu.make_async_copy(SB.at[8 * i + 2 * w + q], AB.at[q, e], rx).start()
                    remote(SB.at[8 * i + 2 * w + 1 - q], AB.at[q, e], sx, rx, e, peer).start()

    GF[0:8] = jnp.zeros((8, 32, 256), F32)
    GF[24:32] = jnp.zeros((8, 32, 256), F32)
    pltpu.make_async_copy(AB, AB, rx).wait()
    pltpu.make_async_copy(SB.at[pl.ds(0, 31)], SB.at[pl.ds(0, 31)], sx).wait()

    for k in range(16):
        GF[8 + k] = AB[1, k].astype(F32)
    for rr in range(4):
        rows = pl.ds(8 * rr, 8)
        lr, li = [], []
        for k in range(16):
            v = AB[0, k, pl.ds(8 * rr, 8), :].astype(F32)
            lr.append(v[:, :128])
            li.append(v[:, 128:])
        for k in range(16):
            LF[k, rows, :] = jnp.concatenate([lr[k], li[k]], axis=1)

    blk, j, h = lax.rem(ey - ex + 4, 4), lax.div(ex, 2), lax.rem(ex, 2)
    home = lax.div(blk, 2)
    dst = out.at[0, lax.rem(blk, 2), j, pl.ds(pl.multiple_of(h * 64 + q * 32, 32), 32), :]
    is_home = home == q

    def far_first(k):
        return jnp.where(k == 3, 0, jnp.where(k == 0, 2, 2 * k - 1))

    def one(n, carry):
        ma = lax.rem(ex + far_first(lax.div(n, 4)), 4)
        mb = lax.rem(ey + far_first(lax.rem(n, 4)), 4)
        m = 4 * ma + mb
        base = 8 - offs[m]
        for rr in range(4):
            rows = pl.ds(8 * rr, 8)
            acc_r = jnp.zeros((8, 128), F32)
            acc_i = jnp.zeros((8, 128), F32)
            for k in range(16):
                lr = LF[k, rows, 0:128]
                li = LF[k, rows, 128:256]
                gr = GF[base + k, rows, 0:128]
                gi = GF[base + k, rows, 128:256]
                acc_r = acc_r + (lr * gr - li * gi)
                acc_i = acc_i + (lr * gi + li * gr)
            OB[m, rows, 0:128] = (acc_r * (1.0 / 16)).astype(BF)
            OB[m, rows, 128:256] = (acc_i * (1.0 / 16)).astype(BF)

        @pl.when(n < 15)
        def _():
            remote(OB.at[m], dst, so, ro, m, 2 * c + home).start()

        return carry

    lax.fori_loop(0, 16, one, 0)

    @pl.when(is_home)
    def _():
        pltpu.make_async_copy(OB.at[e], dst, ro).start()

    @pl.when(jnp.logical_not(is_home))
    def _():
        remote(OB.at[e], dst, so, ro, e, peer).start()

    pltpu.make_async_copy(out, out, ro).wait()

    @pl.when(is_home)
    def _():
        pltpu.make_async_copy(OB.at[pl.ds(0, 15)], OB.at[pl.ds(0, 15)], so).wait()

    @pl.when(jnp.logical_not(is_home))
    def _():
        pltpu.make_async_copy(OB, OB, so).wait()

    p_copy.wait_send()
    t_copy.wait_send()
    j_copy.wait_send()

    @pl.when(a1_sender)
    def _():
        a1.wait_send()

    @pl.when(a1_taker)
    def _():
        a1f.wait_send()

    @pl.when(c == 5)
    def _():
        a2b.wait_send()

    @pl.when(c >= 6)
    def _():
        a2f.wait_send()

    @pl.when(c == 6)
    def _():
        a2r.wait_send()
        for cp in s2r:
            cp.wait_send()

    @pl.when(down_sender)
    def _():
        ad.wait_send()

    @pl.when(mirrored & (c == 2))
    def _():
        ae.wait_send()

    @pl.when(mirrored & (c == 0))
    def _():
        for cp in z2:
            cp.wait_send()

    @pl.when(c == source)
    def _():
        for to in x3:
            for cp in to:
                cp.wait_send()


def shards(retarded, coupling, sigma_lesser, sigma_greater, tiles, offsets):
    mat = (256, 512)
    dma = pltpu.SemaphoreType.DMA
    anyspace = pl.BlockSpec(memory_space=pltpu.HBM)
    return pl.pallas_call(
        kernel,
        out_shape=pltpu.VMEM((1, 2, 2, 128, 256), BF),
        in_specs=[anyspace] * 5 + [pl.BlockSpec(memory_space=pltpu.SMEM)],
        out_specs=pl.BlockSpec(memory_space=pltpu.VMEM),
        scratch_shapes=[
            pltpu.VMEM((2,) + mat, BF), pltpu.VMEM((2,) + mat, BF), pltpu.VMEM((2, 2) + mat, BF),
            pltpu.VMEM((4,) + mat, BF), pltpu.VMEM((8,) + mat, BF), pltpu.VMEM((4,) + mat, BF),
            pltpu.VMEM((2,) + mat, BF), pltpu.VMEM((4,) + mat, BF),
            pltpu.VMEM(mat, BF), pltpu.VMEM(mat, BF),
            pltpu.VMEM(mat, BF), pltpu.VMEM(mat, BF), pltpu.VMEM(mat, BF),
            pltpu.VMEM(mat, BF), pltpu.VMEM(mat, BF), pltpu.VMEM(mat, BF), pltpu.VMEM(mat, BF), pltpu.VMEM(mat, BF),
            pltpu.VMEM((16, 128, 256), BF), pltpu.VMEM((32, 32, 256), BF), pltpu.VMEM((2, 16, 32, 256), BF),
            pltpu.VMEM((16, 32, 256), F32), pltpu.VMEM((32, 32, 256), F32), pltpu.VMEM((16, 32, 256), BF),
            pltpu.SMEM((2, 2, 2), jnp.int32),
            dma((9,)), dma, dma, dma, dma, dma((5,)), dma((4,)), dma((9,)), dma((5,)), dma((4,)), dma((4,)),
            dma((2,)), dma((2,)), dma((16,)), dma((4,)), dma, dma, dma, dma, pltpu.SemaphoreType.REGULAR,
        ],
        compiler_params=pltpu.CompilerParams(
            collective_id=0, has_side_effects=True, vmem_limit_bytes=63 << 20),
        name="recursion",
    )(retarded, coupling, sigma_lesser, sigma_greater, tiles, offsets)


def solution(mesh):
    placed = (
        P("energy", "domain", None, None),
        P("domain", None, None),
        P("energy", "domain", None, None),
        P("energy", "domain", None, None),
        P("domain", None),
        P(),
    )
    return jax.shard_map(
        shards,
        mesh=mesh,
        in_specs=placed,
        out_specs=P("energy", "domain", None, None, None),
        check_vma=False,
    )
```
